512 devices in a mesh: grp: 32 (over y, z_lo, core), sub: 16 (over x, z_hi).
Axes of the slice: x: 4, y: 8, z: 8 (z_hi: 4, z_lo: 2; z = z_hi * 2 + z_lo), core: 2. Of those that a mesh axis runs over, the one named last changes fastest.
Arguments:
- spectra: bfloat16 [2, 6, 32768, 384], P(None, None, ('grp', 'sub'))
- partner_table: int32 [2, 32], replicated, may hold values from 0 to 31, as said below
Outputs:
- group_cross: float32 [2, 6, 32768, 1024], P(None, None, ('grp', 'sub'))
- partner_cross: float32 [2, 2, 6, 2097152], P(None, None, None, ('grp', 'sub'))
The draws below stay inside these ranges and needn't reach their ends.
Inputs may be any that keep to these rules, and one draw needn't show every extreme that they name: partner_table[r, g] = g XOR m_r, where the round's mask m_r (1 to 30) is the same for all groups, and m_1 = m_0 XOR (31).
All inputs are finite; a program needn't handle non-finite values.
Results may differ from the reference program's by a relative error of at most 0.0041.
Values may be sent and summed in bfloat16 or wider, within the bound.
A program may use at most 64 MiB of HBM per device.

```python
import math
import jax
import jax.numpy as jnp
from jax import lax

F = 6
W = 384
CH_DEV = 64
ROUNDS = 2
GROUPS = 32
GROUP_CH = 1024
CHANNELS = 32768


def draw_spectra(key, part):
    base_key, chan_key, window_key = jax.random.split(jax.random.fold_in(key, 11), 3)
    shape_full = (2, F, CHANNELS, W)
    base = jax.random.normal(base_key, shape_full, jnp.float32)
    base = jnp.clip(base, -5.0, 5.0)
    chan_scale = jnp.exp(jax.random.uniform(chan_key, (1, 1, CHANNELS, 1), jnp.float32, 0.0, math.log(10.0)))
    window_scale = jnp.exp(jax.random.uniform(window_key, (1, 1, 1, W), jnp.float32, 0.0, math.log(10.0)))
    return (base * chan_scale * window_scale).astype(jnp.bfloat16)


def draw_partner_table(key, part):
    mask_key = jax.random.fold_in(key, 23)
    first_mask = jax.random.randint(mask_key, (), 1, GROUPS - 1, dtype=jnp.int32)
    second_mask = jnp.bitwise_xor(first_mask, GROUPS - 1)
    groups_all = jnp.arange(GROUPS, dtype=jnp.int32)
    rows_list = []
    for round_num in range(ROUNDS):
        chosen = first_mask if round_num % 2 == 0 else second_mask
        rows_list.append(jnp.bitwise_xor(groups_all, chosen))
    return jnp.stack(rows_list).astype(jnp.int32)


def setup_inputs(seed: int = 0) -> dict:
    arg_keys = jax.random.split(jax.random.key(seed), 3)
    spectra = draw_spectra(jax.random.fold_in(arg_keys[2], 71), 0)
    partner_table = draw_partner_table(jax.random.fold_in(arg_keys[2], 71), 0)
    return dict(spectra=spectra, partner_table=partner_table)


EPSILON = 1e-06

def whiten(spectra):
    values = spectra.astype(jnp.float32)
    power_mean = lax.optimization_barrier(jnp.mean(values[0] * values[0] + values[1] * values[1], axis=0))
    return (values / jnp.sqrt(power_mean + EPSILON)).astype(jnp.bfloat16)

def reference(spectra, partner_table):
    whitened_f32 = whiten(spectra).astype(jnp.float32)
    group_count = CHANNELS // GROUP_CH
    sub_count = GROUP_CH // CH_DEV
    scale = 1.0 / W
    high = lax.Precision.HIGHEST

    def one_group(group_num):
        group_block = lax.dynamic_slice_in_dim(whitened_f32, group_num * GROUP_CH, GROUP_CH, axis=2)
        real_part = jnp.einsum('fcw,fdw->fcd', group_block[0], group_block[0], precision=high)
        real_part = real_part + jnp.einsum('fcw,fdw->fcd', group_block[1], group_block[1], precision=high)
        imag_part = jnp.einsum('fcw,fdw->fcd', group_block[1], group_block[0], precision=high)
        imag_part = imag_part - jnp.einsum('fcw,fdw->fcd', group_block[0], group_block[1], precision=high)
        return jnp.stack([real_part, imag_part]) * scale
    stacked = lax.map(one_group, jnp.arange(group_count, dtype=jnp.int32))
    group_cross = jnp.transpose(stacked, (1, 2, 0, 3, 4)).reshape(2, F, CHANNELS, GROUP_CH)
    blocked = whitened_f32.reshape(2, F, group_count, sub_count, CH_DEV, W)
    results = []
    for round_num in range(ROUNDS):
        partner_block = jnp.take(blocked, partner_table[round_num], axis=2)
        real_part = jnp.einsum('fgscw,fgsdw->fgscd', blocked[0], partner_block[0], precision=high)
        real_part = real_part + jnp.einsum('fgscw,fgsdw->fgscd', blocked[1], partner_block[1], precision=high)
        imag_part = jnp.einsum('fgscw,fgsdw->fgscd', blocked[1], partner_block[0], precision=high)
        imag_part = imag_part - jnp.einsum('fgscw,fgsdw->fgscd', blocked[0], partner_block[1], precision=high)
        results.append((jnp.stack([real_part, imag_part]) * scale).reshape(2, F, CHANNELS * CH_DEV))
    partner_cross = jnp.stack(results)
    return (group_cross, partner_cross)
```

```python
import functools

import jax
import jax.numpy as jnp
from jax import lax
from jax.experimental import pallas as pl
from jax.experimental.pallas import tpu as pltpu
from jax.sharding import PartitionSpec as P

EPSILON = 1e-06
MESH = pl.DeviceIdType.MESH
NX = 4
NZ = 4
NT = (((1,), (1,)), ((), ()))


def flipped(index, mask):
    out = index
    for bit in range(mask.bit_length()):
        if mask >> bit & 1:
            out = out + (1 - 2 * ((index // (1 << bit)) % 2)) * (1 << bit)
    return out


def whiten_kernel(spectra_ref, y_ref):
    values = spectra_ref[...].astype(jnp.float32)
    power_mean = jnp.mean(values[0] * values[0] + values[1] * values[1], axis=0)
    scaled = values * (1.0 / jnp.sqrt(power_mean + EPSILON))
    windows = values.shape[-1]
    y_ref[:, :, :windows] = scaled[0].astype(y_ref.dtype)
    y_ref[:, :, windows:] = scaled[1].astype(y_ref.dtype)


def whiten(spectra):
    _, bins, chans, windows = spectra.shape
    rows = 16
    return pl.pallas_call(
        whiten_kernel,
        grid=(chans // rows,),
        in_specs=[pl.BlockSpec((2, bins, rows, windows), lambda i: (0, 0, i, 0))],
        out_specs=pl.BlockSpec((bins, rows, 2 * windows), lambda i: (0, i, 0)),
        out_shape=jax.ShapeDtypeStruct((bins, chans, 2 * windows), jnp.bfloat16),
        name="whiten",
    )(spectra)


def both_parts(block):
    half = block.shape[1] // 2
    return [block, jnp.concatenate([-block[:, half:], block[:, :half]], axis=1)]


def cross_kernel(
    masks,
    y_ref,
    group_ref,
    partner_ref,
    row,
    col,
    part_in,
    gbuf,
    pbuf,
    to_row,
    to_col,
    to_part,
    own_send,
    own_recv,
    relay_send,
    relay_recv,
    res_send,
    res_recv,
    part_send,
    part_recv,
    pres_send,
    pres_recv,
    out_sem,
):
    bins, chans, depth = y_ref.shape
    half = bins // 2
    scale = 2.0 / depth
    grp = lax.axis_index("grp")
    sub = lax.axis_index("sub")
    x, z = sub // NZ, sub % NZ

    def at(dx, dz):
        return (grp, ((x + dx + NX) % NX) * NZ + (z + dz + NZ) % NZ)

    peers = [(flipped(grp, mask), sub) for mask in masks]
    sides = [(grp // (1 << (mask.bit_length() - 1))) % 2 for mask in masks]

    barrier = pltpu.get_barrier_semaphore()
    greeted = [at(1, 0), at(2, 0), at(3, 0), at(0, 1), at(0, 3)] + peers
    for device in greeted:
        pl.semaphore_signal(barrier, inc=1, device_id=device, device_id_type=MESH)
    pl.semaphore_wait(barrier, len(greeted))

    def remote(src, dst, send, recv, device):
        return pltpu.make_async_remote_copy(
            src_ref=src, dst_ref=dst, send_sem=send, recv_sem=recv, device_id=device, device_id_type=MESH
        )

    def bin_of(step):
        return step // 2 + half * (step % 2), 1 - 2 * (step % 2)

    def own_copies(f, sign):
        return [
            remote(y_ref.at[f], col.at[0, f], own_send.at[0, f], own_recv.at[0, f], at(0, sign)),
            remote(y_ref.at[f], row.at[2, f], own_send.at[1, f], own_recv.at[1, f], at(1, 0)),
            remote(y_ref.at[f], row.at[0, f], own_send.at[2, f], own_recv.at[2, f], at(-1, 0)),
        ]

    def relay_copies(f, sign):
        return [
            remote(col.at[0, f], col.at[1, f], relay_send.at[0, f], relay_recv.at[0, f], at(0, sign)),
            remote(row.at[1 + sign, f], row.at[1, f], relay_send.at[1, f], relay_recv.at[1, f], at(sign, 0)),
        ]

    def result_copies(f, sign):
        copies = [
            remote(
                to_row.at[dx - 1, f],
                gbuf.at[f, pl.ds(2 * NX + 2 * x, 2)],
                res_send.at[dx, f],
                res_recv.at[dx, f],
                at(dx, 0),
            )
            for dx in range(1, NX)
        ]
        copies.append(
            remote(to_col.at[f], gbuf.at[f, pl.ds(0, NX)], res_send.at[0, f], res_recv.at[0, f], at(0, -sign))
        )
        return copies

    def part_copies(r, h):
        return remote(
            y_ref.at[half * (1 - sides[r]) + h],
            part_in.at[r, h],
            part_send.at[r, h],
            part_recv.at[r, h],
            peers[r],
        )

    def part_results(r, h):
        return remote(
            to_part.at[r, h],
            pbuf.at[r, half * sides[r] + h],
            pres_send.at[r, h],
            pres_recv.at[r, h],
            peers[r],
        )

    def product(left, right):
        out = lax.dot_general(
            jnp.concatenate(left, axis=0) if len(left) > 1 else left[0],
            jnp.concatenate([part for block in right for part in both_parts(block)], axis=0),
            NT,
            preferred_element_type=jnp.float32,
        )
        return (out * scale).astype(jnp.bfloat16)

    def send_own(step):
        for copy in own_copies(*bin_of(step)):
            copy.start()

    def relay(step):
        f, sign = bin_of(step)
        own = own_copies(f, sign)
        onward = relay_copies(f, sign)
        own[0].wait_recv()
        onward[0].start()
        own[1].wait_recv()
        own[2].wait_recv()
        onward[1].start()

    def compute(step):
        f, sign = bin_of(step)
        for copy in relay_copies(f, sign):
            copy.wait_recv()
        blocks = [y_ref[f]] + [row[dx - 1, f] for dx in range(1, NX)]
        near, far = col[0, f], col[1, f]
        across = product(blocks, [near, far])
        for dx in range(1, NX):
            rows = across[dx * chans : (dx + 1) * chans]
            to_row[dx - 1, f, 0] = rows[:, : 2 * chans]
            to_row[dx - 1, f, 1] = rows[:, 2 * chans :]
        gbuf[f, 2 * NX + 2 * x] = across[:chans, : 2 * chans]
        gbuf[f, 2 * NX + 2 * x + 1] = across[:chans, 2 * chans :]
        along = product([blocks[0], near], blocks)
        for dx in range(NX):
            place = (x + dx) % NX
            to_col[f, place] = along[chans:, 2 * dx * chans : 2 * (dx + 1) * chans]
        for dx in range(NX):
            place = (x + dx) % NX
            gbuf[f, NX + place] = along[:chans, 2 * dx * chans : 2 * (dx + 1) * chans]
        for copy in result_copies(f, sign):
            copy.start()

    def partner(h):
        for r in range(len(masks)):
            part_copies(r, h).wait_recv()
        for r in range(len(masks)):
            f = half * sides[r] + h
            own, other = y_ref[f], part_in[r, h]
            to_part[r, h] = product([other], [own])
            pbuf[r, f] = product([own], [other])
        for r in range(len(masks)):
            part_results(r, h).start()

    def step_of(n, carry):
        pl.when(n < bins)(lambda: send_own(n))

        @pl.when(n < half)
        def _():
            for r in range(len(masks)):
                part_copies(r, n).start()

        pl.when((n >= 1) & (n < bins + 1))(lambda: relay(n - 1))
        pl.when(n >= 2)(lambda: compute(n - 2))
        pl.when((n >= 3) & (n % 2 == 1))(lambda: partner((n - 3) // 2))
        return carry

    lax.fori_loop(0, bins + 2, step_of, 0)

    def out_copy(f):
        return pltpu.make_async_copy(gbuf.at[f], group_ref.at[f], out_sem.at[f])

    def finish(n, carry):
        f, sign = bin_of(n)
        for copy in result_copies(f, sign):
            copy.wait_recv()
        out_copy(f).start()
        return carry

    lax.fori_loop(0, bins, finish, 0)
    for r in range(len(masks)):
        for h in range(half):
            part_results(r, h).wait_recv()
    last = pltpu.make_async_copy(pbuf, partner_ref, out_sem.at[bins])
    last.start()

    def drain(n, carry):
        f, sign = bin_of(n)
        for copy in own_copies(f, sign) + relay_copies(f, sign) + result_copies(f, sign):
            copy.wait_send()
        out_copy(f).wait()
        return carry

    lax.fori_loop(0, bins, drain, 0)
    for r in range(len(masks)):
        for h in range(half):
            part_copies(r, h).wait_send()
            part_results(r, h).wait_send()
    last.wait()


def cross(y, masks, call):
    bins, chans, depth = y.shape
    half = bins // 2
    wide = 2 * chans
    bf16 = jnp.bfloat16
    dma = pltpu.SemaphoreType.DMA
    return pl.pallas_call(
        functools.partial(cross_kernel, masks),
        in_specs=[pl.BlockSpec(memory_space=pltpu.VMEM)],
        out_specs=[pl.BlockSpec(memory_space=pl.ANY)] * 2,
        out_shape=[
            jax.ShapeDtypeStruct((bins, NX * NZ, chans, wide), bf16),
            jax.ShapeDtypeStruct((2, bins, chans, wide), bf16),
        ],
        scratch_shapes=[
            pltpu.VMEM((NX - 1, bins, chans, depth), bf16),
            pltpu.VMEM((2, bins, chans, depth), bf16),
            pltpu.VMEM((2, half, chans, depth), bf16),
            pltpu.VMEM((bins, NX * NZ, chans, wide), bf16),
            pltpu.VMEM((2, bins, chans, wide), bf16),
            pltpu.VMEM((NX - 1, bins, 2, chans, wide), bf16),
            pltpu.VMEM((bins, NX, chans, wide), bf16),
            pltpu.VMEM((2, half, chans, wide), bf16),
            dma((3, bins)),
            dma((3, bins)),
            dma((2, bins)),
            dma((2, bins)),
            dma((NX, bins)),
            dma((NX, bins)),
            dma((2, half)),
            dma((2, half)),
            dma((2, half)),
            dma((2, half)),
            dma((bins + 1,)),
        ],
        compiler_params=pltpu.CompilerParams(collective_id=call, has_side_effects=True),
        name="cross",
    )(y)


def spread_kernel(near_ref, out_ref):
    bins = pl.num_programs(0)
    chans = near_ref.shape[2]
    z = lax.axis_index("sub") % NZ
    sign = jnp.where(pl.program_id(0) < bins // 2, 1, -1)

    def block_of(xa, za):
        turn = ((z - za) * sign + NZ) % NZ
        slot = jnp.where(
            turn == 0, NX + xa, jnp.where(turn == 1, 2 * NX + 2 * xa, jnp.where(turn == 2, 2 * NX + 2 * xa + 1, xa))
        )
        return near_ref[0, slot].astype(jnp.float32)

    for xa in range(NX):
        for za in range(0, NZ, 2):
            first, second = block_of(xa, za), block_of(xa, za + 1)
            lanes = pl.ds((xa * NZ + za) * chans, 2 * chans)
            out_ref[0, 0, :, lanes] = jnp.concatenate([first[:, :chans], second[:, :chans]], axis=1)
            out_ref[1, 0, :, lanes] = jnp.concatenate([first[:, chans:], second[:, chans:]], axis=1)


def spread(results):
    bins, slots, chans, wide = results.shape
    return pl.pallas_call(
        spread_kernel,
        grid=(bins,),
        in_specs=[pl.BlockSpec((1, slots, chans, wide), lambda f: (f, 0, 0, 0))],
        out_specs=pl.BlockSpec((2, 1, chans, slots * chans), lambda f: (0, f, 0, 0)),
        out_shape=jax.ShapeDtypeStruct((2, bins, chans, slots * chans), jnp.float32),
        name="spread",
    )(results)


def shards(spectra, partner_table):
    y = whiten(spectra)
    bins, chans, _ = y.shape
    groups = lax.axis_size("grp")
    first = partner_table[0, 0]
    low = jnp.minimum(first, groups - 1 - first)
    branches = [
        functools.partial(cross, masks=(mask, groups - 1 - mask), call=mask - 1) for mask in range(1, groups // 2)
    ]
    results, partner = lax.switch(low - 1, branches, y)
    partner = jnp.where(first == low, partner, partner[::-1]).astype(jnp.float32)
    partner = partner.reshape(2, bins, chans, 2, chans).transpose(0, 3, 1, 2, 4)
    return spread(results), partner.reshape(2, 2, bins, chans * chans)


def solution(mesh):
    placed = (P(None, None, ("grp", "sub"), None), P())
    return jax.shard_map(
        shards,
        mesh=mesh,
        in_specs=placed,
        out_specs=(P(None, None, ("grp", "sub"), None), P(None, None, None, ("grp", "sub"))),
        check_vma=False,
    )
```

```python
import functools

import jax
import jax.numpy as jnp
from jax import lax
from jax.experimental import pallas as pl
from jax.experimental.pallas import tpu as pltpu
from jax.sharding import PartitionSpec as P

EPSILON = 1e-06
MESH = pl.DeviceIdType.MESH
NX = 4
NZ = 4
Z_LOW = 2
ROWS = 16
NT = (((1,), (1,)), ((), ()))


def flipped(index, mask):
    out = index
    for bit in range(mask.bit_length()):
        if mask >> bit & 1:
            out = out + (1 - 2 * ((index // (1 << bit)) % 2)) * (1 << bit)
    return out


def both_parts(block):
    half = block.shape[1] // 2
    return [block, jnp.concatenate([-block[:, half:], block[:, :half]], axis=1)]


def cross_kernel(
    masks,
    pieces,
    spectra_ref,
    table_ref,
    group_ref,
    partner_ref,
    y,
    row,
    mid,
    col,
    part_in,
    gbuf,
    pbuf,
    to_row,
    to_col,
    to_part,
    gout,
    pout,
    row_send,
    row_recv,
    col_send,
    col_recv,
    res_send,
    res_recv,
    part_send,
    part_recv,
    out_sem,
    ready,
):
    bins, chans, depth = y.shape
    half = bins // 2
    windows = depth // 2
    wide = 2 * chans
    scale = 1.0 / windows
    rounds = range(len(masks))
    grp = lax.axis_index("grp")
    sub = lax.axis_index("sub")
    x, z = sub // NZ, sub % NZ

    def at(dx, dz):
        return (grp, ((x + dx + NX) % NX) * NZ + (z + dz + NZ) % NZ)

    z_low = (grp // Z_LOW) % 2

    def beside(sign):
        dz = jnp.where(sign > 0, z_low, z_low - 1)
        return (grp + Z_LOW * (1 - 2 * z_low), x * NZ + (z + dz + NZ) % NZ)

    over = [r for r, mask in enumerate(masks) if mask & Z_LOW][0]
    inner = masks[over] - Z_LOW
    peers = [(flipped(grp, mask), sub) for mask in masks]
    sides = [1 - z_low if r == over else (grp // (1 << (mask.bit_length() - 1))) % 2 for r, mask in enumerate(masks)]
    inner_peer = (flipped(grp, inner), sub)

    def bit_of(mask):
        return Z_LOW if mask & Z_LOW else 1 << (mask.bit_length() - 1)

    height = 2 * z + z_low
    meets = [(at(dx, 0), (x + dx) % NX < x, NX - 1 - dx) for dx in range(1, NX)]
    meets += [(at(0, 1), (z + 1) % NZ < z, NX), (at(0, -1), (z + NZ - 1) % NZ < z, NX - 1)]
    meets += [
        (beside(1), (height + 1) % (2 * NZ) < height, NX + 2),
        (beside(-1), (height + 2 * NZ - 1) % (2 * NZ) < height, NX + 1),
    ]
    meets += [
        (peer, (grp // bit_of(mask)) % 2 == 1, NX + 3 + r) for r, (peer, mask) in enumerate(zip(peers, masks))
    ]
    if inner:
        meets.append((inner_peer, (grp // bit_of(inner)) % 2 == 1, NX + 5))
    barrier = pltpu.get_barrier_semaphore()
    callers = 0
    for device, first, _ in meets:
        callers = callers + jnp.where(first, 1, 0)

        @pl.when(jnp.logical_not(first))
        def _(device=device):
            pl.semaphore_signal(barrier, inc=1, device_id=device, device_id_type=MESH)

    def await_ready(k):
        @pl.when(jnp.logical_not(meets[k][1]))
        def _():
            pl.semaphore_wait(ready.at[k], 1)

    def await_beside(way):
        @pl.when((height + 1 - 2 * way + 2 * NZ) % (2 * NZ) > height)
        def _():
            pl.semaphore_wait(ready.at[NX + 1 + way], 1)

    def await_col(way):
        @pl.when((z + 1 - 2 * way + NZ) % NZ > z)
        def _():
            pl.semaphore_wait(ready.at[NX - 1 + way], 1)

    def whiten(i, carry):
        rows = pl.ds(pl.multiple_of(i * ROWS, ROWS), ROWS)
        power = jnp.zeros((ROWS, windows), jnp.float32)
        for f in range(bins):
            real = spectra_ref[0, f, rows].astype(jnp.float32)
            imag = spectra_ref[1, f, rows].astype(jnp.float32)
            power = power + (real * real + imag * imag)
        factor = 1.0 / jnp.sqrt(power / bins + EPSILON)
        for f in range(bins):
            for part in range(2):
                value = spectra_ref[part, f, rows].astype(jnp.float32) * factor
                y[f, rows, part * windows : (part + 1) * windows] = value.astype(y.dtype)
        return carry

    lax.fori_loop(0, chans // ROWS, whiten, 0)
    pl.when(callers > 0)(lambda: pl.semaphore_wait(barrier, callers))
    for device, first, slot in meets:

        @pl.when(first)
        def _(device=device, slot=slot):
            pl.semaphore_signal(ready.at[slot], inc=1, device_id=device, device_id_type=MESH)


    def remote(src, dst, send, recv, device):
        return pltpu.make_async_remote_copy(
            src_ref=src, dst_ref=dst, send_sem=send, recv_sem=recv, device_id=device, device_id_type=MESH
        )

    def sign_of(way):
        return 1 - 2 * way

    def lower_upper(way, start=0, stop=None):
        stop = half if stop is None else stop
        return pl.ds(half * way + start, stop - start)

    def row_own(way, upper, piece):
        f = lower_upper(upper, *pieces[piece])
        return remote(
            y.at[f],
            row.at[(NX - 2) * (1 - way), f],
            row_send.at[way, upper, piece],
            row_recv.at[way, upper, piece],
            at(sign_of(way), 0),
        )

    def row_relay(way, piece):
        f = lower_upper(way, *pieces[piece])
        return remote(
            row.at[(NX - 2) * (1 - way), f],
            row.at[1, f],
            row_send.at[2, way, piece],
            row_recv.at[2, way, piece],
            at(sign_of(way), 0),
        )

    def col_copy(stage, way, piece):
        f = lower_upper(way, *pieces[piece])
        src, dst = ((y.at[f], mid.at[f]), (mid.at[f], col.at[0, f]), (col.at[0, f], col.at[1, f]))[stage]
        sign = sign_of(way)
        return remote(
            src,
            dst,
            col_send.at[stage, way, piece],
            col_recv.at[stage, way, piece],
            at(0, sign) if stage == 2 else beside(sign),
        )

    def bin_of(step):
        return step // 2 + half * (step % 2), 1 - 2 * (step % 2)

    def result_col(f, sign):
        return remote(to_col.at[f], gbuf.at[f, pl.ds(0, NX)], res_send.at[0, f], res_recv.at[0, f], at(0, -sign))

    def results_row(f):
        return [
            remote(
                to_row.at[dx - 1, f],
                gbuf.at[f, pl.ds(2 * NX + 2 * x, 2)],
                res_send.at[dx, f],
                res_recv.at[dx, f],
                at(dx, 0),
            )
            for dx in range(1, NX)
        ]

    def part_own(r, piece):
        start, stop = pieces[piece]
        size = stop - start
        if r == over:
            src, device = mid.at[pl.ds(half * (1 - z_low) + start, size)], inner_peer
        else:
            src, device = y.at[pl.ds(half * (1 - sides[r]) + start, size)], peers[r]
        dst = part_in.at[r, pl.ds(start, size)]
        if r == over and not inner:
            return pltpu.make_async_copy(src, dst, part_recv.at[r, piece])
        return remote(src, dst, part_send.at[r, piece], part_recv.at[r, piece], device)

    def part_await(r, piece):
        copy = part_own(r, piece)
        copy.wait() if r == over and not inner else copy.wait_recv()

    def part_result(r):
        return remote(
            to_part.at[r],
            pbuf.at[r, pl.ds(half * sides[r], half)],
            part_send.at[r, len(pieces)],
            part_recv.at[r, len(pieces)],
            peers[r],
        )

    def product(left, right):
        out = lax.dot_general(
            jnp.concatenate(left, axis=0) if len(left) > 1 else left[0],
            jnp.concatenate([part for block in right for part in both_parts(block)], axis=0),
            NT,
            preferred_element_type=jnp.float32,
        )
        return (out * scale).astype(jnp.bfloat16)

    ways = (jnp.where(height == 0, 0, 1), jnp.where(height == 0, 1, 0))
    await_beside(ways[0])
    col_copy(0, ways[0], 0).start()
    await_ready(0)
    await_ready(NX - 2)
    for way in range(2):
        row_own(way, way, 0).start()
    for way in range(2):
        row_own(way, 1 - way, 0).start()
    await_beside(ways[1])
    col_copy(0, ways[1], 0).start()
    await_ready(NX + 3 + 1 - over)
    for piece in range(len(pieces)):
        part_own(1 - over, piece).start()
    await_ready(NX - 3)
    for piece in range(1, len(pieces)):
        for way in ways:
            col_copy(0, way, piece).start()
        for way in range(2):
            row_own(way, way, piece).start()
    for piece in range(len(pieces)):
        for way in ways:
            col_copy(0, way, piece).wait_recv()
            col_copy(1, way, piece).start()
        if inner and piece == 0:
            await_ready(NX + 5)
        part_own(over, piece).start()
        for way in range(2):
            row_own(way, way, piece).wait_recv()
            row_relay(way, piece).start()
        for way in range(2):
            if piece > 0:
                row_own(way, 1 - way, piece).start()
        for way in ways:
            if piece == 0:
                await_col(way)
            col_copy(1, way, piece).wait_recv()
            col_copy(2, way, piece).start()

    def row_blocks(f):
        return [y[f]] + [row[dx - 1, f] for dx in range(1, NX)]

    def near(f, sign):
        blocks, other = row_blocks(f), col[0, f]
        along = product([blocks[0], other], blocks)
        for dx in range(NX):
            to_col[f, (x + dx) % NX] = along[chans:, dx * wide : (dx + 1) * wide]
        for dx in range(NX):
            gbuf[f, NX + (x + dx) % NX] = along[:chans, dx * wide : (dx + 1) * wide]
        across = product(blocks, [other])
        result_col(f, sign).start()
        for dx in range(1, NX):
            to_row[dx - 1, f, 0] = across[dx * chans : (dx + 1) * chans]
        gbuf[f, 2 * NX + 2 * x] = across[:chans]

    def near_step(n, carry):
        for piece, (start, stop) in enumerate(pieces):

            @pl.when(n == 2 * start)
            def _(piece=piece):
                for way in range(2):
                    row_own(way, 1 - way, piece).wait_recv()
                    row_relay(way, piece).wait_recv()

        near(*bin_of(n))
        return carry

    lax.fori_loop(0, bins, near_step, 0)

    def partner_step(n, carry):
        r, h = n // half, n % half
        f = half * jnp.where(r == 0, sides[0], sides[1]) + h
        own, other = y[f], part_in[r, h]
        to_part[r, h] = product([other], [own])
        pbuf[r, f] = product([own], [other])
        return carry

    def partner():
        for r in rounds:
            for piece in range(len(pieces)):
                part_await(r, piece)
        lax.fori_loop(0, len(masks) * half, partner_step, 0)
        for r in rounds:
            part_result(r).start()

    def far_step(n, carry):
        for piece, (start, stop) in enumerate(pieces):

            @pl.when(n == 2 * start)
            def _(piece=piece):
                if piece == len(pieces) - 1:
                    await_ready(NX + 3 + over)
                    partner()
                for way in range(2):
                    col_copy(2, way, piece).wait_recv()

        f, _ = bin_of(n)
        across = product(row_blocks(f), [col[1, f]])
        for dx in range(1, NX):
            to_row[dx - 1, f, 1] = across[dx * chans : (dx + 1) * chans]
        gbuf[f, 2 * NX + 2 * x + 1] = across[:chans]
        for copy in results_row(f):
            copy.start()
        return carry

    lax.fori_loop(0, bins, far_step, 0)

    for r in rounds:
        part_result(r).wait_recv()
    rows_even = lax.broadcasted_iota(jnp.int32, (chans, wide), 0) % 2 == 0
    lanes_low = lax.broadcasted_iota(jnp.int32, (chans, wide), 1) < chans
    in_order = jnp.broadcast_to(table_ref[0:1, 0:1], (chans, wide)) == masks[0]

    def woven(block):
        block = block.astype(jnp.float32)
        turned = pltpu.roll(block, chans, 1)
        upper = jnp.where(lanes_low, block, pltpu.roll(turned, chans - 1, 0))
        lower = jnp.where(lanes_low, pltpu.roll(turned, 1, 0), block)
        return jnp.where(rows_even, upper, lower)

    def weave(f, carry):
        first, second = woven(pbuf[0, f]), woven(pbuf[1, f])
        for r, block in enumerate((jnp.where(in_order, first, second), jnp.where(in_order, second, first))):
            for pair in range(chans // 2):
                pout[r, f, :, pair * wide : (pair + 1) * wide] = block[2 * pair : 2 * pair + 2]
        return carry

    lax.fori_loop(0, bins, weave, 0)
    partner_out = pltpu.make_async_copy(pout, partner_ref, out_sem.at[bins])
    partner_out.start()

    def group_out(f):
        return pltpu.make_async_copy(gout.at[:, f], group_ref.at[:, f], out_sem.at[f])

    def assemble(n, carry):
        f, sign = bin_of(n)
        for copy in results_row(f):
            copy.wait_recv()
        result_col(f, sign).wait_recv()

        def block_of(xa, za):
            turn = ((z - za) * sign + NZ) % NZ
            slot = jnp.where(
                turn == 0, NX + xa, jnp.where(turn == 1, 2 * NX + 2 * xa, jnp.where(turn == 2, 2 * NX + 2 * xa + 1, xa))
            )
            return gbuf[f, slot].astype(jnp.float32)

        for xa in range(NX):
            for za in range(0, NZ, 2):
                first, second = block_of(xa, za), block_of(xa, za + 1)
                lanes = pl.ds((xa * NZ + za) * chans, wide)
                gout[0, f, :, lanes] = jnp.concatenate([first[:, :chans], second[:, :chans]], axis=1)
                gout[1, f, :, lanes] = jnp.concatenate([first[:, chans:], second[:, chans:]], axis=1)
        group_out(f).start()
        return carry

    lax.fori_loop(0, bins, assemble, 0)


    for way in range(2):
        for piece in range(len(pieces)):
            for stage in range(3):
                col_copy(stage, way, piece).wait_send()
            for upper in range(2):
                row_own(way, upper, piece).wait_send()
            row_relay(way, piece).wait_send()
    for r in rounds:
        for piece in range(len(pieces)):
            if r != over or inner:
                part_own(r, piece).wait_send()
        part_result(r).wait_send()

    def drain(n, carry):
        f, sign = bin_of(n)
        for copy in results_row(f):
            copy.wait_send()
        result_col(f, sign).wait_send()
        group_out(f).wait()
        return carry

    lax.fori_loop(0, bins, drain, 0)
    partner_out.wait()


def cross(spectra, table, masks, call):
    _, bins, chans, windows = spectra.shape
    half = bins // 2
    depth, wide = 2 * windows, 2 * chans
    pieces = ((0, half - 1), (half - 1, half)) if half > 1 else ((0, half),)
    bf16 = jnp.bfloat16
    dma = pltpu.SemaphoreType.DMA
    return pl.pallas_call(
        functools.partial(cross_kernel, masks, pieces),
        in_specs=[pl.BlockSpec(memory_space=pltpu.VMEM)] * 2,
        out_specs=[pl.BlockSpec(memory_space=pl.ANY)] * 2,
        out_shape=[
            jax.ShapeDtypeStruct((2, bins, chans, NX * NZ * chans), jnp.float32),
            jax.ShapeDtypeStruct((2, bins, 2, chans * chans), jnp.float32),
        ],
        scratch_shapes=[
            pltpu.VMEM((bins, chans, depth), bf16),
            pltpu.VMEM((NX - 1, bins, chans, depth), bf16),
            pltpu.VMEM((bins, chans, depth), bf16),
            pltpu.VMEM((2, bins, chans, depth), bf16),
            pltpu.VMEM((2, half, chans, depth), bf16),
            pltpu.VMEM((bins, NX * NZ, chans, wide), bf16),
            pltpu.VMEM((2, bins, chans, wide), bf16),
            pltpu.VMEM((NX - 1, bins, 2, chans, wide), bf16),
            pltpu.VMEM((bins, NX, chans, wide), bf16),
            pltpu.VMEM((2, half, chans, wide), bf16),
            pltpu.VMEM((2, bins, chans, NX * NZ * chans), jnp.float32),
            pltpu.VMEM((2, bins, 2, chans * chans), jnp.float32),
            dma((3, 2, len(pieces))),
            dma((3, 2, len(pieces))),
            dma((3, 2, len(pieces))),
            dma((3, 2, len(pieces))),
            dma((NX, bins)),
            dma((NX, bins)),
            dma((2, len(pieces) + 1)),
            dma((2, len(pieces) + 1)),
            dma((bins + 1,)),
            pltpu.SemaphoreType.REGULAR((NX + 6,)),
        ],
        compiler_params=pltpu.CompilerParams(collective_id=call, has_side_effects=True),
        name="cross",
    )(spectra, table)


def shards(spectra, partner_table):
    groups = lax.axis_size("grp")
    first = partner_table[0, 0]
    low = jnp.minimum(first, groups - 1 - first)
    branches = [
        functools.partial(cross, masks=(mask, groups - 1 - mask), call=mask - 1) for mask in range(1, groups // 2)
    ]
    group_cross, partner = lax.switch(low - 1, branches, spectra, partner_table)
    return group_cross, partner.transpose(0, 2, 1, 3)


def solution(mesh):
    placed = (P(None, None, ("grp", "sub"), None), P())
    return jax.shard_map(
        shards,
        mesh=mesh,
        in_specs=placed,
        out_specs=(P(None, None, ("grp", "sub"), None), P(None, None, None, ("grp", "sub"))),
        check_vma=False,
    )
```

```python
import functools

import jax
import jax.numpy as jnp
from jax import lax
from jax.experimental import pallas as pl
from jax.experimental.pallas import tpu as pltpu
from jax.sharding import PartitionSpec as P

EPSILON = 1e-06
MESH = pl.DeviceIdType.MESH
NX = 4
NZ = 4
Z_LOW = 2
ROWS = 16
NT = (((1,), (1,)), ((), ()))


def flipped(index, mask):
    out = index
    for bit in range(mask.bit_length()):
        if mask >> bit & 1:
            out = out + (1 - 2 * ((index // (1 << bit)) % 2)) * (1 << bit)
    return out


def both_parts(block):
    half = block.shape[1] // 2
    return [block, jnp.concatenate([-block[:, half:], block[:, :half]], axis=1)]


def cross_kernel(
    masks,
    pieces,
    spectra_ref,
    table_ref,
    group_ref,
    partner_ref,
    y,
    row,
    mid,
    col,
    part_in,
    gbuf,
    pbuf,
    to_row,
    to_col,
    to_part,
    gout,
    pout,
    row_send,
    row_recv,
    col_send,
    col_recv,
    res_send,
    res_recv,
    part_send,
    part_recv,
    out_sem,
    ready,
):
    bins, chans, depth = y.shape
    half = bins // 2
    windows = depth // 2
    wide = 2 * chans
    scale = 1.0 / windows
    rounds = range(len(masks))
    grp = lax.axis_index("grp")
    sub = lax.axis_index("sub")
    x, z = sub // NZ, sub % NZ

    def at(dx, dz):
        return (grp, ((x + dx + NX) % NX) * NZ + (z + dz + NZ) % NZ)

    z_low = (grp // Z_LOW) % 2

    def beside(sign):
        dz = jnp.where(sign > 0, z_low, z_low - 1)
        return (grp + Z_LOW * (1 - 2 * z_low), x * NZ + (z + dz + NZ) % NZ)

    over = [r for r, mask in enumerate(masks) if mask & Z_LOW][0]
    inner = masks[over] - Z_LOW
    peers = [(flipped(grp, mask), sub) for mask in masks]
    sides = [1 - z_low if r == over else (grp // (1 << (mask.bit_length() - 1))) % 2 for r, mask in enumerate(masks)]
    inner_peer = (flipped(grp, inner), sub)

    def bit_of(mask):
        return Z_LOW if mask & Z_LOW else 1 << (mask.bit_length() - 1)

    height = 2 * z + z_low
    meets = [(at(dx, 0), (x + dx) % NX < x, NX - 1 - dx) for dx in range(1, NX)]
    meets += [(at(0, 1), (z + 1) % NZ < z, NX), (at(0, -1), (z + NZ - 1) % NZ < z, NX - 1)]
    meets += [
        (beside(1), (height + 1) % (2 * NZ) < height, NX + 2),
        (beside(-1), (height + 2 * NZ - 1) % (2 * NZ) < height, NX + 1),
    ]
    meets += [
        (peer, (grp // bit_of(mask)) % 2 == 1, NX + 3 + r) for r, (peer, mask) in enumerate(zip(peers, masks))
    ]
    if inner:
        meets.append((inner_peer, (grp // bit_of(inner)) % 2 == 1, NX + 5))
    barrier = pltpu.get_barrier_semaphore()
    callers = 0
    for device, first, _ in meets:
        callers = callers + jnp.where(first, 1, 0)

        @pl.when(jnp.logical_not(first))
        def _(device=device):
            pl.semaphore_signal(barrier, inc=1, device_id=device, device_id_type=MESH)

    def await_ready(k):
        @pl.when(jnp.logical_not(meets[k][1]))
        def _():
            pl.semaphore_wait(ready.at[k], 1)

    def await_beside(way):
        @pl.when((height + 1 - 2 * way + 2 * NZ) % (2 * NZ) > height)
        def _():
            pl.semaphore_wait(ready.at[NX + 1 + way], 1)

    def await_col(way):
        @pl.when((z + 1 - 2 * way + NZ) % NZ > z)
        def _():
            pl.semaphore_wait(ready.at[NX - 1 + way], 1)

    def whiten(i, carry):
        rows = pl.ds(pl.multiple_of(i * ROWS, ROWS), ROWS)
        power = jnp.zeros((ROWS, windows), jnp.float32)
        for f in range(bins):
            real = spectra_ref[0, f, rows].astype(jnp.float32)
            imag = spectra_ref[1, f, rows].astype(jnp.float32)
            power = power + (real * real + imag * imag)
        factor = 1.0 / jnp.sqrt(power / bins + EPSILON)
        for f in range(bins):
            for part in range(2):
                value = spectra_ref[part, f, rows].astype(jnp.float32) * factor
                y[f, rows, part * windows : (part + 1) * windows] = value.astype(y.dtype)
        return carry

    lax.fori_loop(0, chans // ROWS, whiten, 0)
    pl.when(callers > 0)(lambda: pl.semaphore_wait(barrier, callers))
    for device, first, slot in meets:

        @pl.when(first)
        def _(device=device, slot=slot):
            pl.semaphore_signal(ready.at[slot], inc=1, device_id=device, device_id_type=MESH)


    def remote(src, dst, send, recv, device):
        return pltpu.make_async_remote_copy(
            src_ref=src, dst_ref=dst, send_sem=send, recv_sem=recv, device_id=device, device_id_type=MESH
        )

    def sign_of(way):
        return 1 - 2 * way

    def lower_upper(way, start=0, stop=None):
        stop = half if stop is None else stop
        return pl.ds(half * way + start, stop - start)

    def row_own(way, upper, piece):
        f = lower_upper(upper, *pieces[piece])
        return remote(
            y.at[f],
            row.at[(NX - 2) * (1 - way), f],
            row_send.at[way, upper, piece],
            row_recv.at[way, upper, piece],
            at(sign_of(way), 0),
        )

    def row_relay(way, piece):
        f = lower_upper(way, *pieces[piece])
        return remote(
            row.at[(NX - 2) * (1 - way), f],
            row.at[1, f],
            row_send.at[2, way, piece],
            row_recv.at[2, way, piece],
            at(sign_of(way), 0),
        )

    def col_copy(stage, way, piece):
        f = lower_upper(way, *pieces[piece])
        src, dst = ((y.at[f], mid.at[f]), (mid.at[f], col.at[0, f]), (col.at[0, f], col.at[1, f]))[stage]
        sign = sign_of(way)
        return remote(
            src,
            dst,
            col_send.at[stage, way, piece],
            col_recv.at[stage, way, piece],
            at(0, sign) if stage == 2 else beside(sign),
        )

    def bin_of(step):
        return step // 2 + half * (step % 2), 1 - 2 * (step % 2)

    def result_col(f, sign):
        return remote(to_col.at[f], gbuf.at[f, pl.ds(0, NX)], res_send.at[0, f], res_recv.at[0, f], at(0, -sign))

    def results_row(f):
        return [
            remote(
                to_row.at[dx - 1, f],
                gbuf.at[f, pl.ds(2 * NX + 2 * x, 2)],
                res_send.at[dx, f],
                res_recv.at[dx, f],
                at(dx, 0),
            )
            for dx in range(1, NX)
        ]

    def part_own(r, piece):
        start, stop = pieces[piece]
        size = stop - start
        if r == over:
            src, device = mid.at[pl.ds(half * (1 - z_low) + start, size)], inner_peer
        else:
            src, device = y.at[pl.ds(half * (1 - sides[r]) + start, size)], peers[r]
        dst = part_in.at[r, pl.ds(start, size)]
        if r == over and not inner:
            return pltpu.make_async_copy(src, dst, part_recv.at[r, piece])
        return remote(src, dst, part_send.at[r, piece], part_recv.at[r, piece], device)

    def part_await(r, piece):
        copy = part_own(r, piece)
        copy.wait() if r == over and not inner else copy.wait_recv()

    def part_result(r):
        return remote(
            to_part.at[r],
            pbuf.at[r, pl.ds(half * sides[r], half)],
            part_send.at[r, len(pieces)],
            part_recv.at[r, len(pieces)],
            peers[r],
        )

    def product(left, right):
        out = lax.dot_general(
            jnp.concatenate(left, axis=0) if len(left) > 1 else left[0],
            jnp.concatenate([part for block in right for part in both_parts(block)], axis=0),
            NT,
            preferred_element_type=jnp.float32,
        )
        return (out * scale).astype(jnp.bfloat16)

    ways = (jnp.where(height == 0, 0, 1), jnp.where(height == 0, 1, 0))
    await_beside(ways[0])
    col_copy(0, ways[0], 0).start()
    await_ready(0)
    await_ready(NX - 2)
    for way in range(2):
        row_own(way, way, 0).start()
    for way in range(2):
        row_own(way, 1 - way, 0).start()
    await_beside(ways[1])
    col_copy(0, ways[1], 0).start()
    await_ready(NX + 3 + 1 - over)
    for piece in range(len(pieces)):
        part_own(1 - over, piece).start()
    await_ready(NX - 3)
    for piece in range(1, len(pieces)):
        for way in ways:
            col_copy(0, way, piece).start()
        for way in range(2):
            row_own(way, way, piece).start()

    def onward(piece):
        for way in ways:
            if piece == 0:
                await_col(way)
            col_copy(1, way, piece).wait_recv()
            col_copy(2, way, piece).start()

    for piece in range(len(pieces)):
        for way in ways:
            col_copy(0, way, piece).wait_recv()
            col_copy(1, way, piece).start()
        if inner and piece == 0:
            await_ready(NX + 5)
        part_own(over, piece).start()
        for way in range(2):
            row_own(way, way, piece).wait_recv()
            row_relay(way, piece).start()
            if piece + 1 < len(pieces):
                row_own(way, 1 - way, piece + 1).start()
        if piece > 0:
            onward(piece - 1)
    onward(len(pieces) - 1)

    def row_blocks(f):
        return [y[f]] + [row[dx - 1, f] for dx in range(1, NX)]

    def near(f, sign):
        blocks, other = row_blocks(f), col[0, f]
        along = product([blocks[0], other], blocks)
        for dx in range(NX):
            to_col[f, (x + dx) % NX] = along[chans:, dx * wide : (dx + 1) * wide]
        for dx in range(NX):
            gbuf[f, NX + (x + dx) % NX] = along[:chans, dx * wide : (dx + 1) * wide]
        across = product(blocks, [other])
        result_col(f, sign).start()
        for dx in range(1, NX):
            to_row[dx - 1, f, 0] = across[dx * chans : (dx + 1) * chans]
        gbuf[f, 2 * NX + 2 * x] = across[:chans]

    def near_step(n, carry):
        for piece, (start, stop) in enumerate(pieces):

            @pl.when(n == 2 * start)
            def _(piece=piece):
                for way in range(2):
                    row_own(way, 1 - way, piece).wait_recv()
                    row_relay(way, piece).wait_recv()

        near(*bin_of(n))
        return carry

    lax.fori_loop(0, bins, near_step, 0)

    def partner_step(n, carry):
        r, h = n // half, n % half
        f = half * jnp.where(r == 0, sides[0], sides[1]) + h
        own, other = y[f], part_in[r, h]
        to_part[r, h] = product([other], [own])
        pbuf[r, f] = product([own], [other])
        return carry

    def partner():
        for r in rounds:
            for piece in range(len(pieces)):
                part_await(r, piece)
        lax.fori_loop(0, len(masks) * half, partner_step, 0)
        for r in rounds:
            part_result(r).start()

    def far_step(n, carry):
        for piece, (start, stop) in enumerate(pieces):

            @pl.when(n == 2 * start)
            def _(piece=piece):
                if piece == len(pieces) - 1:
                    await_ready(NX + 3 + over)
                    partner()
                for way in range(2):
                    col_copy(2, way, piece).wait_recv()

        f, _ = bin_of(n)
        across = product(row_blocks(f), [col[1, f]])
        for dx in range(1, NX):
            to_row[dx - 1, f, 1] = across[dx * chans : (dx + 1) * chans]
        gbuf[f, 2 * NX + 2 * x + 1] = across[:chans]
        for copy in results_row(f):
            copy.start()
        return carry

    lax.fori_loop(0, bins, far_step, 0)

    for r in rounds:
        part_result(r).wait_recv()
    rows_even = lax.broadcasted_iota(jnp.int32, (chans, wide), 0) % 2 == 0
    lanes_low = lax.broadcasted_iota(jnp.int32, (chans, wide), 1) < chans
    in_order = jnp.broadcast_to(table_ref[0:1, 0:1], (chans, wide)) == masks[0]

    def woven(block):
        block = block.astype(jnp.float32)
        turned = pltpu.roll(block, chans, 1)
        upper = jnp.where(lanes_low, block, pltpu.roll(turned, chans - 1, 0))
        lower = jnp.where(lanes_low, pltpu.roll(turned, 1, 0), block)
        return jnp.where(rows_even, upper, lower)

    def weave(f, carry):
        first, second = woven(pbuf[0, f]), woven(pbuf[1, f])
        for r, block in enumerate((jnp.where(in_order, first, second), jnp.where(in_order, second, first))):
            for pair in range(chans // 2):
                pout[r, f, :, pair * wide : (pair + 1) * wide] = block[2 * pair : 2 * pair + 2]
        return carry

    lax.fori_loop(0, bins, weave, 0)
    partner_out = pltpu.make_async_copy(pout, partner_ref, out_sem.at[bins])
    partner_out.start()

    def group_out(f):
        return pltpu.make_async_copy(gout.at[:, f], group_ref.at[:, f], out_sem.at[f])

    def assemble(n, carry):
        f, sign = bin_of(n)
        for copy in results_row(f):
            copy.wait_recv()
        result_col(f, sign).wait_recv()

        def block_of(xa, za):
            turn = ((z - za) * sign + NZ) % NZ
            slot = jnp.where(
                turn == 0, NX + xa, jnp.where(turn == 1, 2 * NX + 2 * xa, jnp.where(turn == 2, 2 * NX + 2 * xa + 1, xa))
            )
            return gbuf[f, slot].astype(jnp.float32)

        for xa in range(NX):
            for za in range(0, NZ, 2):
                first, second = block_of(xa, za), block_of(xa, za + 1)
                lanes = pl.ds((xa * NZ + za) * chans, wide)
                gout[0, f, :, lanes] = jnp.concatenate([first[:, :chans], second[:, :chans]], axis=1)
                gout[1, f, :, lanes] = jnp.concatenate([first[:, chans:], second[:, chans:]], axis=1)
        group_out(f).start()
        return carry

    lax.fori_loop(0, bins, assemble, 0)


    for way in range(2):
        for piece in range(len(pieces)):
            for stage in range(3):
                col_copy(stage, way, piece).wait_send()
            for upper in range(2):
                row_own(way, upper, piece).wait_send()
            row_relay(way, piece).wait_send()
    for r in rounds:
        for piece in range(len(pieces)):
            if r != over or inner:
                part_own(r, piece).wait_send()
        part_result(r).wait_send()

    def drain(n, carry):
        f, sign = bin_of(n)
        for copy in results_row(f):
            copy.wait_send()
        result_col(f, sign).wait_send()
        group_out(f).wait()
        return carry

    lax.fori_loop(0, bins, drain, 0)
    partner_out.wait()


def cross(spectra, table, masks, call):
    _, bins, chans, windows = spectra.shape
    half = bins // 2
    depth, wide = 2 * windows, 2 * chans
    pieces = tuple((f, f + 1) for f in range(half))
    bf16 = jnp.bfloat16
    dma = pltpu.SemaphoreType.DMA
    return pl.pallas_call(
        functools.partial(cross_kernel, masks, pieces),
        in_specs=[pl.BlockSpec(memory_space=pltpu.VMEM)] * 2,
        out_specs=[pl.BlockSpec(memory_space=pl.ANY)] * 2,
        out_shape=[
            jax.ShapeDtypeStruct((2, bins, chans, NX * NZ * chans), jnp.float32),
            jax.ShapeDtypeStruct((2, bins, 2, chans * chans), jnp.float32),
        ],
        scratch_shapes=[
            pltpu.VMEM((bins, chans, depth), bf16),
            pltpu.VMEM((NX - 1, bins, chans, depth), bf16),
            pltpu.VMEM((bins, chans, depth), bf16),
            pltpu.VMEM((2, bins, chans, depth), bf16),
            pltpu.VMEM((2, half, chans, depth), bf16),
            pltpu.VMEM((bins, NX * NZ, chans, wide), bf16),
            pltpu.VMEM((2, bins, chans, wide), bf16),
            pltpu.VMEM((NX - 1, bins, 2, chans, wide), bf16),
            pltpu.VMEM((bins, NX, chans, wide), bf16),
            pltpu.VMEM((2, half, chans, wide), bf16),
            pltpu.VMEM((2, bins, chans, NX * NZ * chans), jnp.float32),
            pltpu.VMEM((2, bins, 2, chans * chans), jnp.float32),
            dma((3, 2, len(pieces))),
            dma((3, 2, len(pieces))),
            dma((3, 2, len(pieces))),
            dma((3, 2, len(pieces))),
            dma((NX, bins)),
            dma((NX, bins)),
            dma((2, len(pieces) + 1)),
            dma((2, len(pieces) + 1)),
            dma((bins + 1,)),
            pltpu.SemaphoreType.REGULAR((NX + 6,)),
        ],
        compiler_params=pltpu.CompilerParams(collective_id=call, has_side_effects=True),
        name="cross",
    )(spectra, table)


def shards(spectra, partner_table):
    groups = lax.axis_size("grp")
    first = partner_table[0, 0]
    low = jnp.minimum(first, groups - 1 - first)
    branches = [
        functools.partial(cross, masks=(mask, groups - 1 - mask), call=mask - 1) for mask in range(1, groups // 2)
    ]
    group_cross, partner = lax.switch(low - 1, branches, spectra, partner_table)
    return group_cross, partner.transpose(0, 2, 1, 3)


def solution(mesh):
    placed = (P(None, None, ("grp", "sub"), None), P())
    return jax.shard_map(
        shards,
        mesh=mesh,
        in_specs=placed,
        out_specs=(P(None, None, ("grp", "sub"), None), P(None, None, None, ("grp", "sub"))),
        check_vma=False,
    )
```
